32 devices in a mesh: sec: 16 (over z, y, x), tile: 2 (over core).
Axes of the slice: x: 2, y: 2, z: 4, core: 2. Of those that a mesh axis runs over, the one named last changes fastest.
Arguments:
- probe: float32 [2, 16, 512], P(None, 'tile'), may hold values from -5 to 5
- offsets: int32 [4], replicated, may hold values from 0 to 511
- phase: float32 [32, 16, 512], P('sec', 'tile'), may hold values from -1.5 to 1.5
- absorption: float32 [32, 16, 512], P('sec', 'tile'), may hold values from 0 to 0.02
- measured: float32 [4, 16, 512], P(None, 'tile'), may hold values from 0.2 to 2
Outputs:
- gradient: float32 [32, 2, 16, 512], P('sec', None, 'tile')
The draws below stay inside these ranges and needn't reach their ends.
All inputs are finite; a program needn't handle non-finite values.
Results may differ from the reference program's by a relative error of at most 0.00013.
Values sent between devices are 32-bit elements; how exact they have to be, the bound alone decides.
A program may use at most 64 MiB of HBM per device.

```python
import jax
import jax.numpy as jnp
from jax import lax

COLS = 512
PROBES = 4
N_ROWS = 16
SLICES = 32


def draw_offsets(key, part):
    values = jax.random.randint(jax.random.fold_in(key, 11), (PROBES,), 0, COLS)
    chosen = jax.random.randint(jax.random.fold_in(key, 12), (), 0, PROBES)
    values = values.at[chosen].set(COLS - 1)
    return values.astype(jnp.int32)


def steps_of(own_key, extent, pieces, low, top_value):
    level = 1.0
    for axis_at, blocks in pieces:
        draws = jax.random.uniform(jax.random.fold_in(jax.random.fold_in(own_key, 6), axis_at), (blocks,), jnp.float32, low / len(pieces), top_value / len(pieces))
        level = level * jnp.repeat(jnp.exp(draws), extent[axis_at] // blocks).reshape((-1,) + (1,) * (len(extent) - 1 - axis_at))
    return level


def gaussian(stream_key, shape, deviation, limit, cuts=(), kind=jnp.bfloat16):
    loudness = steps_of(stream_key, shape, cuts, -0.22, 0.18) if cuts else 1.0
    array = jax.random.normal(stream_key, shape, jnp.float32) * deviation * loudness
    return jnp.minimum(jnp.maximum(array, -limit), limit).astype(kind)


def setup_inputs(seed: int = 0) -> dict:
    splits = jax.random.split(jax.random.key(seed), 6)
    probe = gaussian(splits[0], (2, N_ROWS, COLS), 1.0, 5.0, ((1, 2),), jnp.float32)
    offsets = draw_offsets(jax.random.fold_in(splits[5], 71), 0)
    phase = gaussian(splits[2], (SLICES, N_ROWS, COLS), 0.3, 1.5, ((0, 16), (1, 2)), jnp.float32)
    absorption = jnp.clip(0.02 * jax.random.uniform(splits[3], (SLICES, N_ROWS, COLS), jnp.float32) ** steps_of(splits[3], (SLICES, N_ROWS, COLS), ((0, 16), (1, 2)), -0.2, 0.2), 0.0, 0.02)
    measured = jnp.clip(0.2 + 1.8 * jax.random.uniform(splits[4], (PROBES, N_ROWS, COLS), jnp.float32) ** steps_of(splits[4], (PROBES, N_ROWS, COLS), ((1, 2),), -0.2, 0.2), 0.2, 2.0)
    return {"probe": probe, "offsets": offsets, "phase": phase, "absorption": absorption, "measured": measured}


PROP_RE = 0.004
PROP_IM = 0.0314

def complex_product(multiplier, operand):
    real_part = multiplier[..., 0, :, :] * operand[..., 0, :, :] - multiplier[..., 1, :, :] * operand[..., 1, :, :]
    imag_part = multiplier[..., 0, :, :] * operand[..., 1, :, :] + multiplier[..., 1, :, :] * operand[..., 0, :, :]
    return jnp.stack([real_part, imag_part], -3)

def propagate_rows(wavefield):
    extended = jnp.pad(wavefield, ((0, 0), (1, 1), (0, 0)))
    laplacian = extended[:, :-2] + extended[:, 2:] + jnp.roll(wavefield, 1, -1) + jnp.roll(wavefield, -1, -1) - 4.0 * wavefield
    real_part = wavefield[0] + PROP_RE * laplacian[0] - PROP_IM * laplacian[1]
    imag_part = wavefield[1] + PROP_RE * laplacian[1] + PROP_IM * laplacian[0]
    return jnp.stack([real_part, imag_part], 0)

def exit_wave(transmission, launched):

    def advance(wavefield, layer_values):
        return (propagate_rows(complex_product(layer_values, wavefield)), None)
    final_wave, unused = lax.scan(advance, launched, transmission)
    return final_wave

def misfit(transmission, probe, offsets, measured):
    launched = jax.vmap(lambda shift_amount: jnp.roll(probe, shift_amount, axis=-1))(offsets)
    exit_waves = jax.vmap(exit_wave, in_axes=(None, 0))(transmission, launched)
    intensity = exit_waves[:, 0] ** 2 + exit_waves[:, 1] ** 2
    return 0.5 * jnp.sum((intensity - measured) ** 2)

def reference(probe, offsets, phase, absorption, measured):
    amplitude = jnp.exp(-absorption)
    transmission = jnp.stack([amplitude * jnp.cos(phase), amplitude * jnp.sin(phase)], 1)
    return jax.grad(misfit)(transmission, probe, offsets, measured)
```

```python
import functools

import jax
import jax.numpy as jnp
from jax import lax
from jax.experimental import pallas as pl
from jax.experimental.pallas import tpu as pltpu
from jax.sharding import PartitionSpec as P

PROP_RE = 0.004
PROP_IM = 0.0314


def padded(value, sides, width):
    for axis, dim in sides:
        size, length = (lax.axis_size(axis), value.shape[dim])
        up = [(i, (i + 1) % size) for i in range(size - 1)]
        down = [(j, i) for i, j in up]
        last = lax.slice_in_dim(value, length - width, length, axis=dim)
        initial = lax.slice_in_dim(value, 0, width, axis=dim)
        before = lax.ppermute(last, axis, up)
        after = lax.ppermute(initial, axis, down)
        value = jnp.concatenate([before, value, after], axis=dim)
    return value


def passed_along(value, axis, steps):
    count = lax.axis_size(axis)
    initial, last = (max(0, -steps), min(count, count - steps))
    return lax.ppermute(value, axis, [(source, source + steps) for source in range(initial, last)])


def complex_product(multiplier, operand):
    real_part = (
        multiplier[..., 0, :, :] * operand[..., 0, :, :]
        - multiplier[..., 1, :, :] * operand[..., 1, :, :]
    )
    imag_part = (
        multiplier[..., 0, :, :] * operand[..., 1, :, :]
        + multiplier[..., 1, :, :] * operand[..., 0, :, :]
    )
    return jnp.stack([real_part, imag_part], -3)


def conjugate_product(multiplier, operand):
    real_part = (
        multiplier[..., 0, :, :] * operand[..., 0, :, :]
        + multiplier[..., 1, :, :] * operand[..., 1, :, :]
    )
    imag_part = (
        multiplier[..., 0, :, :] * operand[..., 1, :, :]
        - multiplier[..., 1, :, :] * operand[..., 0, :, :]
    )
    return jnp.stack([real_part, imag_part], -3)


def propagate(extended, coupling):
    centre = extended[..., 1:-1, :]
    laplacian = (
        extended[..., :-2, :]
        + extended[..., 2:, :]
        + jnp.roll(centre, 1, -1)
        + jnp.roll(centre, -1, -1)
        - 4.0 * centre
    )
    real_part = (
        centre[..., 0, :, :]
        + PROP_RE * laplacian[..., 0, :, :]
        - coupling * laplacian[..., 1, :, :]
    )
    imag_part = (
        centre[..., 1, :, :]
        + PROP_RE * laplacian[..., 1, :, :]
        + coupling * laplacian[..., 0, :, :]
    )
    return jnp.stack([real_part, imag_part], -3)


def forward_section(wavefield, transmission):
    slice_count = transmission.shape[0]
    inputs = []
    for layer_index in range(slice_count):
        inputs.append(wavefield)
        product = complex_product(transmission[layer_index], wavefield)
        extended = padded(product, (("tile", 2),), 1)
        wavefield = propagate(extended, PROP_IM)
    return (jnp.stack(inputs, 1), wavefield)


def backward_section(adjoint, inputs, weight, transmission):
    slice_count = transmission.shape[0]
    slice_grads = [None] * slice_count
    scaled = weight[:, None, None, None]
    for layer_index in reversed(range(slice_count)):
        extended = padded(adjoint, (("tile", 2),), 1)
        adjoint_wave = propagate(extended, -PROP_IM)
        slice_grads[layer_index] = jnp.sum(
            scaled * conjugate_product(inputs[:, layer_index], adjoint_wave), 0
        )
        adjoint = conjugate_product(transmission[layer_index], adjoint_wave)
    return (adjoint, jnp.stack(slice_grads, 0))


def pipelined_body(probe, offsets, phase, absorption, measured):
    slice_count, row_count, col_count = phase.shape
    amplitude = jnp.exp(-absorption)
    transmission = jnp.stack([amplitude * jnp.cos(phase), amplitude * jnp.sin(phase)], 1)
    sections = lax.axis_size("sec")
    section = lax.axis_index("sec")
    probe_count = offsets.shape[0]
    batch_size = 1
    step_count = sections + probe_count - 1

    def plan(step_index, offset_steps):
        raw_ids = (step_index - offset_steps)[None]
        active = (raw_ids >= 0) & (raw_ids < probe_count)
        return (jnp.clip(raw_ids, 0, probe_count - 1), active)

    def launch(shift_amount):
        return jnp.roll(probe, shift_amount, axis=-1)

    def forward_step(step_index, state_carry):
        incoming, stored, exit_waves = state_carry
        probe_ids, active = plan(step_index, section)
        launched = jax.vmap(launch)(offsets[probe_ids])
        wavefield = jnp.where(section == 0, launched, incoming)
        inputs, outgoing = forward_section(wavefield, transmission)
        stored = stored.at[probe_ids].set(
            jnp.where(active[:, None, None, None, None], inputs, stored[probe_ids])
        )
        exit_waves = exit_waves.at[probe_ids].set(
            jnp.where(active[:, None, None, None], outgoing, exit_waves[probe_ids])
        )
        incoming = passed_along(outgoing, "sec", 1)
        return (incoming, stored, exit_waves)

    zero_field = jnp.zeros((batch_size, 2, row_count, col_count), jnp.float32)
    stored = jnp.zeros((probe_count, slice_count, 2, row_count, col_count), jnp.float32)
    exit_waves = jnp.zeros((probe_count, 2, row_count, col_count), jnp.float32)
    unused, stored, exit_waves = lax.fori_loop(
        0, step_count, forward_step, (zero_field, stored, exit_waves)
    )

    def backward_step(step_index, state_carry):
        incoming, gradient = state_carry
        probe_ids, active = plan(step_index, sections - 1 - section)
        exit_part = exit_waves[probe_ids]
        intensity = exit_part[:, 0] ** 2 + exit_part[:, 1] ** 2
        seed_adjoint = 2.0 * (intensity - measured[probe_ids])[:, None] * exit_part
        adjoint = jnp.where(section == sections - 1, seed_adjoint, incoming)
        weight = active.astype(jnp.float32)
        adjoint, gradient_terms = backward_section(adjoint, stored[probe_ids], weight, transmission)
        incoming = passed_along(adjoint, "sec", -1)
        return (incoming, gradient + gradient_terms)

    gradient = jnp.zeros((slice_count, 2, row_count, col_count), jnp.float32)
    unused, gradient = lax.fori_loop(0, step_count, backward_step, (zero_field, gradient))
    return gradient


LANES = 128
SUBLANES = 8
MESH = pl.DeviceIdType.MESH
CENTRE_RE = 1.0 - 4.0 * PROP_RE
CENTRE_IM = -4.0 * PROP_IM
RATIO = complex(PROP_RE, PROP_IM) / complex(CENTRE_RE, CENTRE_IM)


def windowed(sections, tiles, slice_count, row_count, col_count, probe_count):
    groups = col_count // LANES
    return (
        col_count % LANES == 0
        and groups >= 2
        and groups % 2 == 0
        and sections % groups == 0
        and row_count % SUBLANES == 0
        and probe_count % tiles == 0
        and 2 * sections * slice_count <= LANES // 2
        and tiles * row_count <= 4 * SUBLANES
    )


def window_kernel(
    sections, tiles,
    probe_ref, offsets_ref, phase_ref, absorption_ref, measured_ref, out_ref,
    own, field, probes, frames, waves, adjoint, partial, returned,
    group_send, block_recv, plane_send, tile_send, tile_recv,
    aux_send, aux_recv, back_send, back_recv,
):
    slice_count, row_count, col_count = phase_ref.shape
    groups = col_count // LANES
    plane = sections // groups
    width = 2 * LANES
    height = tiles * row_count
    share = frames.shape[1]
    me = lax.axis_index("sec")
    tile = lax.axis_index("tile")
    group, place = lax.div(me, plane), lax.rem(me, plane)
    sent = []

    def device(section, core):
        return {"sec": section, "tile": core}

    def group_at(step):
        return lax.rem(group + step, groups)

    def place_at(step):
        return lax.rem(place + step, plane)

    def tile_at(step):
        return lax.rem(tile + step, tiles)

    def send(source, target, send_sem, recv_sem, section, core):
        copy = pltpu.make_async_remote_copy(
            src_ref=source, dst_ref=target, send_sem=send_sem, recv_sem=recv_sem,
            device_id=device(section, core), device_id_type=MESH,
        )
        copy.start()
        sent.append(copy)

    def arrived(target, recv_sem):
        pltpu.make_async_remote_copy(
            src_ref=target, dst_ref=target, send_sem=recv_sem, recv_sem=recv_sem,
            device_id=device(me, tile), device_id_type=MESH,
        ).wait_recv()

    barrier = pltpu.get_barrier_semaphore()
    partners = 0
    for dz in range(groups):
        for dj in range(tiles):
            if dz or dj:
                pl.semaphore_signal(
                    barrier, inc=1, device_id=device(group_at(dz) * plane + place, tile_at(dj)),
                    device_id_type=MESH,
                )
                partners += 1
    for dq in range(1, plane):
        pl.semaphore_signal(
            barrier, inc=1, device_id=device(group * plane + place_at(dq), tile), device_id_type=MESH
        )
        partners += 1

    for layer in range(slice_count):
        amplitude = jnp.exp(-absorption_ref[layer])
        real = amplitude * jnp.cos(phase_ref[layer])
        imag = amplitude * jnp.sin(phase_ref[layer])
        for part, value in enumerate(
            (CENTRE_RE * real - CENTRE_IM * imag, CENTRE_RE * imag + CENTRE_IM * real)
        ):
            own[layer, part, :, :col_count] = value
            own[layer, part, :, col_count:] = value[:, :LANES]
    start = pl.multiple_of(group * LANES, LANES)
    field[me, tile] = own[:, :, :, pl.ds(start, width)]
    probes[tile] = probe_ref[...]
    frames[tile] = measured_ref[pl.ds(tile * share, share)]
    pl.semaphore_wait(barrier, partners)

    step = 1 - 2 * lax.div(2 * group, groups)
    near = [lax.rem(group + dz * step + groups, groups) for dz in range(groups)]
    for dz in range(groups - 1, 0, -1):
        target = near[dz]
        window = pl.ds(pl.multiple_of(target * LANES, LANES), width)
        send(
            own.at[:, :, :, window], field.at[me, tile], group_send.at[dz], block_recv.at[me],
            target * plane + place, tile,
        )

    def to_plane(dz):
        block = near[dz] * plane + place
        for dq in range(1, plane):
            send(
                field.at[block, tile], field.at[block, tile], plane_send.at[dz, dq],
                block_recv.at[block], group * plane + place_at(dq), tile,
            )

    def to_tiles(block, dz, dq):
        for dj in range(1, tiles):
            send(
                field.at[block, tile], field.at[block, tile], tile_send.at[dz, dq, dj],
                tile_recv.at[block, tile], me, tile_at(dj),
            )

    to_plane(0)
    for dj in range(1, tiles):
        other = tile_at(dj)
        send(probe_ref, probes.at[tile], aux_send.at[0, dj], aux_recv.at[0, tile], me, other)
        send(
            measured_ref.at[pl.ds(other * share, share)], frames.at[tile], aux_send.at[1, dj],
            aux_recv.at[1, tile], me, other,
        )
    to_tiles(me, 0, 0)

    for dj in range(1, tiles):
        other = tile_at(dj)
        arrived(probes.at[other], aux_recv.at[0, other])
        arrived(frames.at[other], aux_recv.at[1, other])
    for index in range(share):
        shift = lax.rem(
            offsets_ref[tile * share + index] + col_count - group * LANES, col_count
        )
        for part in range(2):
            value = jnp.concatenate([probes[t, part] for t in range(tiles)], 0)
            for bit in range((col_count - 1).bit_length()):
                chosen = jnp.full(value.shape, lax.shift_right_logical(shift, bit) & 1) == 1
                value = jnp.where(chosen, pltpu.roll(value, 1 << bit, 1), value)
            waves[0, index, part] = value[:, :width]

    def collect(dz):
        for dq in range(1, plane):
            block = near[dz] * plane + place_at(dq)
            arrived(field.at[block, tile], block_recv.at[block])
            to_tiles(block, dz, dq)

    for dz in range(1, groups):
        block = near[dz] * plane + place
        arrived(field.at[block, tile], block_recv.at[block])
        to_plane(dz)
        to_tiles(block, dz, 0)
        collect(dz - 1)
    collect(groups - 1)

    rows = lax.broadcasted_iota(jnp.int32, (height, width), 0)
    first, last = rows == 0, rows == height - 1

    def neighbours(value):
        above = jnp.where(first, 0.0, pltpu.roll(value, 1, 0))
        below = jnp.where(last, 0.0, pltpu.roll(value, height - 1, 0))
        return (above + below) + (pltpu.roll(value, 1, 1) + pltpu.roll(value, width - 1, 1))

    def spread(real, imag, ratio):
        real_sum, imag_sum = neighbours(real), neighbours(imag)
        return (
            real + (ratio.real * real_sum - ratio.imag * imag_sum),
            imag + (ratio.real * imag_sum + ratio.imag * real_sum),
        )

    def layer_of(block, layer):
        return [
            jnp.concatenate([field[block, t, layer, part] for t in range(tiles)], 0)
            for part in range(2)
        ]

    def forward(block, carry):
        for dj in range(1, tiles):
            other = tile_at(dj)
            arrived(field.at[block, other], tile_recv.at[block, other])
        for layer in range(slice_count):
            at = block * slice_count + layer
            real, imag = layer_of(block, layer)
            for index in range(share):
                wave_re, wave_im = waves[at, index, 0], waves[at, index, 1]
                wave_re, wave_im = spread(
                    real * wave_re - imag * wave_im, real * wave_im + imag * wave_re, RATIO
                )
                waves[at + 1, index, 0] = wave_re
                waves[at + 1, index, 1] = wave_im
        return carry

    lax.fori_loop(0, sections, forward, 0)

    following = pl.multiple_of(group_at(1) * LANES, LANES)
    for index in range(share):
        frame = jnp.concatenate(
            [
                jnp.concatenate([frames[t, index, :, pl.ds(at, LANES)] for t in range(tiles)], 0)
                for at in (start, following)
            ],
            1,
        )
        wave_re, wave_im = (waves[sections * slice_count, index, part] for part in range(2))
        residual = 2.0 * (wave_re * wave_re + wave_im * wave_im - frame)
        adjoint[index, 0] = residual * wave_re
        adjoint[index, 1] = residual * wave_im

    def return_copy(piece, core):
        return pltpu.make_async_remote_copy(
            src_ref=partial.at[piece, core], dst_ref=returned.at[group, tile],
            send_sem=back_send.at[piece, core], recv_sem=back_recv.at[group, tile],
            device_id=device(piece * plane + place, core), device_id_type=MESH,
        )

    def backward(count, carry):
        block = sections - 1 - count
        piece = lax.div(block, plane)
        wanted = lax.rem(block, plane) == place
        for layer in reversed(range(slice_count)):
            at = block * slice_count + layer
            real, imag = layer_of(block, layer)
            backs = []
            for index in range(share):
                back_re, back_im = spread(adjoint[index, 0], adjoint[index, 1], RATIO.conjugate())
                backs.append((back_re, back_im))
                adjoint[index, 0] = real * back_re + imag * back_im
                adjoint[index, 1] = real * back_im - imag * back_re

            @pl.when(wanted)
            def _():
                total_re = total_im = 0.0
                for index, (back_re, back_im) in enumerate(backs):
                    wave_re, wave_im = waves[at, index, 0], waves[at, index, 1]
                    total_re += wave_re * back_re + wave_im * back_im
                    total_im += wave_re * back_im - wave_im * back_re
                for part, total in enumerate((total_re, total_im)):
                    chunk = pltpu.roll(total, width - LANES // 2, 1)[:, :LANES]
                    for core in range(tiles):
                        partial[piece, core, layer, part] = chunk[
                            core * row_count : (core + 1) * row_count
                        ]

        for core in range(tiles):
            @pl.when(wanted & (piece * tiles + core != group * tiles + tile))
            def _():
                return_copy(piece, core).start()

        return carry

    lax.fori_loop(0, sections - place, backward, 0)

    returned[group, tile] = partial[group, tile]
    for dz in range(groups):
        for dj in range(tiles):
            if dz or dj:
                piece, core = group_at(dz), tile_at(dj)
                arrived(returned.at[piece, core], back_recv.at[piece, core])
    for layer in range(slice_count):
        parts = []
        for part in range(2):
            chunks = []
            for piece in range(groups):
                chunk = returned[piece, 0, layer, part]
                for core in range(1, tiles):
                    chunk = chunk + returned[piece, core, layer, part]
                chunks.append(chunk)
            parts.append(pltpu.roll(jnp.concatenate(chunks, 1), LANES // 2, 1))
        real, imag = parts
        out_ref[layer, 0] = CENTRE_RE * real + CENTRE_IM * imag
        out_ref[layer, 1] = CENTRE_RE * imag - CENTRE_IM * real

    for dz in range(groups):
        for dj in range(tiles):
            if dz or dj:
                return_copy(group_at(dz), tile_at(dj)).wait_send()
    for copy in sent:
        copy.wait_send()


def windowed_body(sections, tiles, probe, offsets, phase, absorption, measured):
    slice_count, row_count, col_count = phase.shape
    probe_count = offsets.shape[0]
    groups = col_count // LANES
    plane = sections // groups
    width, height, share = 2 * LANES, tiles * row_count, probe_count // tiles
    vmem = pl.BlockSpec(memory_space=pltpu.VMEM)
    dma = pltpu.SemaphoreType.DMA
    return pl.pallas_call(
        functools.partial(window_kernel, sections, tiles),
        out_shape=jax.ShapeDtypeStruct((slice_count, 2, row_count, col_count), jnp.float32),
        in_specs=[vmem, pl.BlockSpec(memory_space=pltpu.SMEM), vmem, vmem, vmem],
        out_specs=vmem,
        scratch_shapes=[
            pltpu.VMEM((slice_count, 2, row_count, col_count + LANES), jnp.float32),
            pltpu.VMEM((sections, tiles, slice_count, 2, row_count, width), jnp.float32),
            pltpu.VMEM((tiles, 2, row_count, col_count), jnp.float32),
            pltpu.VMEM((tiles, share, row_count, col_count), jnp.float32),
            pltpu.VMEM((sections * slice_count + 1, share, 2, height, width), jnp.float32),
            pltpu.VMEM((share, 2, height, width), jnp.float32),
            pltpu.VMEM((groups, tiles, slice_count, 2, row_count, LANES), jnp.float32),
            pltpu.VMEM((groups, tiles, slice_count, 2, row_count, LANES), jnp.float32),
            dma((groups,)),
            dma((sections,)),
            dma((groups, plane)),
            dma((groups, plane, tiles)),
            dma((sections, tiles)),
            dma((2, tiles)),
            dma((2, tiles)),
            dma((groups, tiles)),
            dma((groups, tiles)),
        ],
        compiler_params=pltpu.CompilerParams(collective_id=0, has_side_effects=True),
    )(probe, offsets, phase, absorption, measured)


def body(probe, offsets, phase, absorption, measured):
    sections, tiles = lax.axis_size("sec"), lax.axis_size("tile")
    if windowed(sections, tiles, *phase.shape, offsets.shape[0]):
        return windowed_body(sections, tiles, probe, offsets, phase, absorption, measured)
    return pipelined_body(probe, offsets, phase, absorption, measured)


def solution(mesh):
    in_specs = (
        P(None, "tile", None),
        P(),
        P("sec", "tile", None),
        P("sec", "tile", None),
        P(None, "tile", None),
    )
    out_specs = P("sec", None, "tile", None)
    return jax.shard_map(body, mesh=mesh, in_specs=in_specs, out_specs=out_specs, check_vma=False)
```

```python
import functools

import jax
import jax.numpy as jnp
from jax import lax
from jax.experimental import pallas as pl
from jax.experimental.pallas import tpu as pltpu
from jax.sharding import PartitionSpec as P

PROP_RE = 0.004
PROP_IM = 0.0314


def padded(value, sides, width):
    for axis, dim in sides:
        size, length = (lax.axis_size(axis), value.shape[dim])
        up = [(i, (i + 1) % size) for i in range(size - 1)]
        down = [(j, i) for i, j in up]
        last = lax.slice_in_dim(value, length - width, length, axis=dim)
        initial = lax.slice_in_dim(value, 0, width, axis=dim)
        before = lax.ppermute(last, axis, up)
        after = lax.ppermute(initial, axis, down)
        value = jnp.concatenate([before, value, after], axis=dim)
    return value


def passed_along(value, axis, steps):
    count = lax.axis_size(axis)
    initial, last = (max(0, -steps), min(count, count - steps))
    return lax.ppermute(value, axis, [(source, source + steps) for source in range(initial, last)])


def complex_product(multiplier, operand):
    real_part = (
        multiplier[..., 0, :, :] * operand[..., 0, :, :]
        - multiplier[..., 1, :, :] * operand[..., 1, :, :]
    )
    imag_part = (
        multiplier[..., 0, :, :] * operand[..., 1, :, :]
        + multiplier[..., 1, :, :] * operand[..., 0, :, :]
    )
    return jnp.stack([real_part, imag_part], -3)


def conjugate_product(multiplier, operand):
    real_part = (
        multiplier[..., 0, :, :] * operand[..., 0, :, :]
        + multiplier[..., 1, :, :] * operand[..., 1, :, :]
    )
    imag_part = (
        multiplier[..., 0, :, :] * operand[..., 1, :, :]
        - multiplier[..., 1, :, :] * operand[..., 0, :, :]
    )
    return jnp.stack([real_part, imag_part], -3)


def propagate(extended, coupling):
    centre = extended[..., 1:-1, :]
    laplacian = (
        extended[..., :-2, :]
        + extended[..., 2:, :]
        + jnp.roll(centre, 1, -1)
        + jnp.roll(centre, -1, -1)
        - 4.0 * centre
    )
    real_part = (
        centre[..., 0, :, :]
        + PROP_RE * laplacian[..., 0, :, :]
        - coupling * laplacian[..., 1, :, :]
    )
    imag_part = (
        centre[..., 1, :, :]
        + PROP_RE * laplacian[..., 1, :, :]
        + coupling * laplacian[..., 0, :, :]
    )
    return jnp.stack([real_part, imag_part], -3)


def forward_section(wavefield, transmission):
    slice_count = transmission.shape[0]
    inputs = []
    for layer_index in range(slice_count):
        inputs.append(wavefield)
        product = complex_product(transmission[layer_index], wavefield)
        extended = padded(product, (("tile", 2),), 1)
        wavefield = propagate(extended, PROP_IM)
    return (jnp.stack(inputs, 1), wavefield)


def backward_section(adjoint, inputs, weight, transmission):
    slice_count = transmission.shape[0]
    slice_grads = [None] * slice_count
    scaled = weight[:, None, None, None]
    for layer_index in reversed(range(slice_count)):
        extended = padded(adjoint, (("tile", 2),), 1)
        adjoint_wave = propagate(extended, -PROP_IM)
        slice_grads[layer_index] = jnp.sum(
            scaled * conjugate_product(inputs[:, layer_index], adjoint_wave), 0
        )
        adjoint = conjugate_product(transmission[layer_index], adjoint_wave)
    return (adjoint, jnp.stack(slice_grads, 0))


def pipelined_body(probe, offsets, phase, absorption, measured):
    slice_count, row_count, col_count = phase.shape
    amplitude = jnp.exp(-absorption)
    transmission = jnp.stack([amplitude * jnp.cos(phase), amplitude * jnp.sin(phase)], 1)
    sections = lax.axis_size("sec")
    section = lax.axis_index("sec")
    probe_count = offsets.shape[0]
    batch_size = 1
    step_count = sections + probe_count - 1

    def plan(step_index, offset_steps):
        raw_ids = (step_index - offset_steps)[None]
        active = (raw_ids >= 0) & (raw_ids < probe_count)
        return (jnp.clip(raw_ids, 0, probe_count - 1), active)

    def launch(shift_amount):
        return jnp.roll(probe, shift_amount, axis=-1)

    def forward_step(step_index, state_carry):
        incoming, stored, exit_waves = state_carry
        probe_ids, active = plan(step_index, section)
        launched = jax.vmap(launch)(offsets[probe_ids])
        wavefield = jnp.where(section == 0, launched, incoming)
        inputs, outgoing = forward_section(wavefield, transmission)
        stored = stored.at[probe_ids].set(
            jnp.where(active[:, None, None, None, None], inputs, stored[probe_ids])
        )
        exit_waves = exit_waves.at[probe_ids].set(
            jnp.where(active[:, None, None, None], outgoing, exit_waves[probe_ids])
        )
        incoming = passed_along(outgoing, "sec", 1)
        return (incoming, stored, exit_waves)

    zero_field = jnp.zeros((batch_size, 2, row_count, col_count), jnp.float32)
    stored = jnp.zeros((probe_count, slice_count, 2, row_count, col_count), jnp.float32)
    exit_waves = jnp.zeros((probe_count, 2, row_count, col_count), jnp.float32)
    unused, stored, exit_waves = lax.fori_loop(
        0, step_count, forward_step, (zero_field, stored, exit_waves)
    )

    def backward_step(step_index, state_carry):
        incoming, gradient = state_carry
        probe_ids, active = plan(step_index, sections - 1 - section)
        exit_part = exit_waves[probe_ids]
        intensity = exit_part[:, 0] ** 2 + exit_part[:, 1] ** 2
        seed_adjoint = 2.0 * (intensity - measured[probe_ids])[:, None] * exit_part
        adjoint = jnp.where(section == sections - 1, seed_adjoint, incoming)
        weight = active.astype(jnp.float32)
        adjoint, gradient_terms = backward_section(adjoint, stored[probe_ids], weight, transmission)
        incoming = passed_along(adjoint, "sec", -1)
        return (incoming, gradient + gradient_terms)

    gradient = jnp.zeros((slice_count, 2, row_count, col_count), jnp.float32)
    unused, gradient = lax.fori_loop(0, step_count, backward_step, (zero_field, gradient))
    return gradient


LANES = 128
SUBLANES = 8
MESH = pl.DeviceIdType.MESH
CENTRE_RE = 1.0 - 4.0 * PROP_RE
CENTRE_IM = -4.0 * PROP_IM
RATIO = complex(PROP_RE, PROP_IM) / complex(CENTRE_RE, CENTRE_IM)


def windowed(sections, tiles, slice_count, row_count, col_count, probe_count):
    groups = col_count // LANES
    return (
        col_count % LANES == 0
        and groups >= 2
        and groups % 2 == 0
        and sections == 4 * groups
        and row_count % SUBLANES == 0
        and probe_count % tiles == 0
        and 2 * sections * slice_count <= LANES // 2
        and tiles * row_count <= 4 * SUBLANES
    )


def window_kernel(
    sections, tiles,
    probe_ref, offsets_ref, phase_ref, absorption_ref, measured_ref, out_ref,
    chain, field, probes, frames, waves, adjoint, partial, returned, shifts,
    chain_send, chain_recv, plane_send, block_recv, corner_send, corner_recv,
    tile_send, tile_recv, aux_send, aux_recv, back_send, back_recv, shift_sem,
):
    slice_count, row_count, col_count = phase_ref.shape
    groups = col_count // LANES
    plane = sections // groups
    width = 2 * LANES
    height = tiles * row_count
    share = frames.shape[1]
    me = lax.axis_index("sec")
    tile = lax.axis_index("tile")
    group, place = lax.div(me, plane), lax.rem(me, plane)
    across = (place + 1 - 2 * lax.rem(place, 2), place + 2 - 4 * lax.div(place, 2))
    corner = plane - 1 - place

    def device(section, core):
        return {"sec": section, "tile": core}

    def group_at(step):
        return lax.rem(group + step, groups)

    def tile_at(step):
        return lax.rem(tile + step, tiles)

    def remote(source, target, send_sem, recv_sem, section, core):
        return pltpu.make_async_remote_copy(
            src_ref=source, dst_ref=target, send_sem=send_sem, recv_sem=recv_sem,
            device_id=device(section, core), device_id_type=MESH,
        )

    def arrived(target, recv_sem):
        remote(target, target, recv_sem, recv_sem, me, tile).wait_recv()

    shift_copy = pltpu.make_async_copy(offsets_ref, shifts, shift_sem)
    shift_copy.start()

    def greet(section, core):
        pl.semaphore_signal(
            pltpu.get_barrier_semaphore(), inc=1, device_id=device(section, core), device_id_type=MESH
        )

    for direction in (1, -1):
        @pl.when((group + direction >= 0) & (group + direction < groups))
        def _():
            greet(me + direction * plane, tile)
    for other in across:
        greet(group * plane + other, tile)
    for dj in range(1, tiles):
        greet(me, tile_at(dj))

    for layer in range(slice_count):
        amplitude = jnp.exp(-absorption_ref[layer])
        real = amplitude * jnp.cos(phase_ref[layer])
        imag = amplitude * jnp.sin(phase_ref[layer])
        for part, value in enumerate(
            (CENTRE_RE * real - CENTRE_IM * imag, CENTRE_RE * imag + CENTRE_IM * real)
        ):
            chain[group, layer, part, :, :col_count] = value
            chain[group, layer, part, :, col_count:] = value[:, :LANES]
    probes[tile] = probe_ref[...]
    frames[tile] = measured_ref[pl.ds(tile * share, share)]
    ends = lax.div(group + groups - 1, groups) + lax.div(2 * groups - 2 - group, groups)
    pl.semaphore_wait(pltpu.get_barrier_semaphore(), tiles - 1 + len(across) + ends)

    def span(at, direction):
        return pl.ds((at + 1) * LANES, (groups - at) * LANES) if direction > 0 else pl.ds(0, (at + 1) * LANES)

    def hop(source, at, direction):
        part = chain.at[source, :, :, :, span(at, direction)]
        return remote(
            part, part, chain_send.at[source, (direction + 1) // 2], chain_recv.at[source],
            me + direction * plane, tile,
        )

    def hops(at):
        for source in range(groups):
            if source <= at < groups - 1:
                yield hop(source, at, 1)
            if source >= at > 0:
                yield hop(source, at, -1)

    def plane_copy(source, view, axis):
        block = source * plane + place
        return remote(
            view, field.at[block, tile], plane_send.at[source, axis], block_recv.at[block],
            group * plane + across[axis], tile,
        )

    def corner_copy(source, axis):
        part = field.at[source * plane + across[axis], tile, :, axis]
        return remote(
            part, part, corner_send.at[source, axis], corner_recv.at[source, axis],
            group * plane + across[1 - axis], tile,
        )

    def tile_copies(block, view):
        return [
            remote(
                view, field.at[block, tile], tile_send.at[block, dj], tile_recv.at[block, tile],
                me, tile_at(dj),
            )
            for dj in range(1, tiles)
        ]

    def aux_copies():
        for dj in range(1, tiles):
            other = tile_at(dj)
            yield remote(
                probe_ref, probes.at[tile], aux_send.at[0, dj], aux_recv.at[0, tile], me, other
            )
            yield remote(
                measured_ref.at[pl.ds(other * share, share)], frames.at[tile], aux_send.at[1, dj],
                aux_recv.at[1, tile], me, other,
            )

    def launch():
        for dj in range(1, tiles):
            other = tile_at(dj)
            arrived(probes.at[other], aux_recv.at[0, other])
            arrived(frames.at[other], aux_recv.at[1, other])
        shift_copy.wait()
        for index in range(share):
            shift = lax.rem(shifts[tile * share + index] + col_count - group * LANES, col_count)
            for part in range(2):
                value = jnp.concatenate([probes[t, part] for t in range(tiles)], 0)
                for bit in range((col_count - 1).bit_length()):
                    chosen = jnp.full(value.shape, lax.shift_right_logical(shift, bit) & 1) == 1
                    value = jnp.where(chosen, pltpu.roll(value, 1 << bit, 1), value)
                waves[0, index, part] = value[:, :width]

    def gather(at):
        window = pl.ds(at * LANES, width)
        order = sorted(range(groups), key=lambda source: (abs(source - at), source))

        def spread_out(source):
            if source <= at < groups - 1:
                hop(source, at, 1).start()
            if source >= at > 0:
                hop(source, at, -1).start()
            view = chain.at[source, :, :, :, window]
            for axis in range(2):
                plane_copy(source, view, axis).start()
            for copy in tile_copies(source * plane + place, view):
                copy.start()
            field[source * plane + place, tile] = chain[source, :, :, :, window]

        def collect(source):
            for axis in range(2):
                block = source * plane + across[axis]
                arrived(field.at[block, tile], block_recv.at[block])
                corner_copy(source, axis).start()
                for copy in tile_copies(block, field.at[block, tile]):
                    copy.start()

        def collect_corner(source):
            block = source * plane + corner
            for axis in range(2):
                arrived(field.at[block, tile, :, axis], corner_recv.at[source, axis])
            for copy in tile_copies(block, field.at[block, tile]):
                copy.start()

        for count in range(groups + 2):
            if count < groups:
                source = order[count]
                if source < at:
                    arrived(chain.at[source, :, :, :, span(at - 1, 1)], chain_recv.at[source])
                if source > at:
                    arrived(chain.at[source, :, :, :, span(at + 1, -1)], chain_recv.at[source])
                spread_out(source)
            if count == 0:
                for copy in aux_copies():
                    copy.start()
            if 0 <= count - 1 < groups:
                collect(order[count - 1])
            if 0 <= count - 2 < groups:
                collect_corner(order[count - 2])
            if count == 0:
                launch()

    for at in range(groups):
        @pl.when(group == at)
        def _():
            gather(at)

    rows = lax.broadcasted_iota(jnp.int32, (height, width), 0)
    first, last = rows == 0, rows == height - 1

    def neighbours(value):
        above = jnp.where(first, 0.0, pltpu.roll(value, 1, 0))
        below = jnp.where(last, 0.0, pltpu.roll(value, height - 1, 0))
        return (above + below) + (pltpu.roll(value, 1, 1) + pltpu.roll(value, width - 1, 1))

    def spread(real, imag, ratio):
        real_sum, imag_sum = neighbours(real), neighbours(imag)
        return (
            real + (ratio.real * real_sum - ratio.imag * imag_sum),
            imag + (ratio.real * imag_sum + ratio.imag * real_sum),
        )

    def layer_of(block, layer):
        return [
            jnp.concatenate([field[block, t, layer, part] for t in range(tiles)], 0)
            for part in range(2)
        ]

    def forward(block, carry):
        for dj in range(1, tiles):
            other = tile_at(dj)
            arrived(field.at[block, other], tile_recv.at[block, other])
        for layer in range(slice_count):
            at = block * slice_count + layer
            real, imag = layer_of(block, layer)
            for index in range(share):
                wave_re, wave_im = waves[at, index, 0], waves[at, index, 1]
                wave_re, wave_im = spread(
                    real * wave_re - imag * wave_im, real * wave_im + imag * wave_re, RATIO
                )
                waves[at + 1, index, 0] = wave_re
                waves[at + 1, index, 1] = wave_im
        return carry

    lax.fori_loop(0, sections, forward, 0)

    start = pl.multiple_of(group * LANES, LANES)
    following = pl.multiple_of(group_at(1) * LANES, LANES)
    for index in range(share):
        frame = jnp.concatenate(
            [
                jnp.concatenate([frames[t, index, :, pl.ds(at, LANES)] for t in range(tiles)], 0)
                for at in (start, following)
            ],
            1,
        )
        wave_re, wave_im = (waves[sections * slice_count, index, part] for part in range(2))
        residual = 2.0 * (wave_re * wave_re + wave_im * wave_im - frame)
        adjoint[index, 0] = residual * wave_re
        adjoint[index, 1] = residual * wave_im

    def return_copy(piece, core):
        return pltpu.make_async_remote_copy(
            src_ref=partial.at[piece, core], dst_ref=returned.at[group, tile],
            send_sem=back_send.at[piece, core], recv_sem=back_recv.at[group, tile],
            device_id=device(piece * plane + place, core), device_id_type=MESH,
        )

    def backward(count, carry):
        block = sections - 1 - count
        piece = lax.div(block, plane)
        wanted = lax.rem(block, plane) == place
        for layer in reversed(range(slice_count)):
            at = block * slice_count + layer
            real, imag = layer_of(block, layer)
            backs = []
            for index in range(share):
                back_re, back_im = spread(adjoint[index, 0], adjoint[index, 1], RATIO.conjugate())
                backs.append((back_re, back_im))
                adjoint[index, 0] = real * back_re + imag * back_im
                adjoint[index, 1] = real * back_im - imag * back_re

            @pl.when(wanted)
            def _():
                total_re = total_im = 0.0
                for index, (back_re, back_im) in enumerate(backs):
                    wave_re, wave_im = waves[at, index, 0], waves[at, index, 1]
                    total_re += wave_re * back_re + wave_im * back_im
                    total_im += wave_re * back_im - wave_im * back_re
                for part, total in enumerate((total_re, total_im)):
                    chunk = pltpu.roll(total, width - LANES // 2, 1)[:, :LANES]
                    for core in range(tiles):
                        partial[piece, core, layer, part] = chunk[
                            core * row_count : (core + 1) * row_count
                        ]

        for core in range(tiles):
            @pl.when(wanted & (piece * tiles + core != group * tiles + tile))
            def _():
                return_copy(piece, core).start()

        return carry

    lax.fori_loop(0, sections - place, backward, 0)

    returned[group, tile] = partial[group, tile]
    for dz in range(groups):
        for dj in range(tiles):
            if dz or dj:
                piece, core = group_at(dz), tile_at(dj)
                arrived(returned.at[piece, core], back_recv.at[piece, core])
    for layer in range(slice_count):
        parts = []
        for part in range(2):
            chunks = []
            for piece in range(groups):
                chunk = returned[piece, 0, layer, part]
                for core in range(1, tiles):
                    chunk = chunk + returned[piece, core, layer, part]
                chunks.append(chunk)
            parts.append(pltpu.roll(jnp.concatenate(chunks, 1), LANES // 2, 1))
        real, imag = parts
        out_ref[layer, 0] = CENTRE_RE * real + CENTRE_IM * imag
        out_ref[layer, 1] = CENTRE_RE * imag - CENTRE_IM * real

    for dz in range(groups):
        for dj in range(tiles):
            if dz or dj:
                return_copy(group_at(dz), tile_at(dj)).wait_send()
    for at in range(groups):
        @pl.when(group == at)
        def _():
            for copy in hops(at):
                copy.wait_send()
    for source in range(groups):
        for axis in range(2):
            plane_copy(source, field.at[source * plane + place, tile], axis).wait_send()
            corner_copy(source, axis).wait_send()
    for block in range(sections):
        for copy in tile_copies(block, field.at[block, tile]):
            copy.wait_send()
    for copy in aux_copies():
        copy.wait_send()


def windowed_body(sections, tiles, probe, offsets, phase, absorption, measured):
    slice_count, row_count, col_count = phase.shape
    probe_count = offsets.shape[0]
    groups = col_count // LANES
    plane = sections // groups
    width, height, share = 2 * LANES, tiles * row_count, probe_count // tiles
    vmem = pl.BlockSpec(memory_space=pltpu.VMEM)
    dma = pltpu.SemaphoreType.DMA
    return pl.pallas_call(
        functools.partial(window_kernel, sections, tiles),
        out_shape=jax.ShapeDtypeStruct((slice_count, 2, row_count, col_count), jnp.float32),
        in_specs=[vmem, pl.BlockSpec(memory_space=pl.ANY), vmem, vmem, vmem],
        out_specs=vmem,
        scratch_shapes=[
            pltpu.VMEM((groups, slice_count, 2, row_count, col_count + LANES), jnp.float32),
            pltpu.VMEM((sections, tiles, slice_count, 2, row_count, width), jnp.float32),
            pltpu.VMEM((tiles, 2, row_count, col_count), jnp.float32),
            pltpu.VMEM((tiles, share, row_count, col_count), jnp.float32),
            pltpu.VMEM((sections * slice_count + 1, share, 2, height, width), jnp.float32),
            pltpu.VMEM((share, 2, height, width), jnp.float32),
            pltpu.VMEM((groups, tiles, slice_count, 2, row_count, LANES), jnp.float32),
            pltpu.VMEM((groups, tiles, slice_count, 2, row_count, LANES), jnp.float32),
            pltpu.SMEM((probe_count,), jnp.int32),
            dma((groups, 2)),
            dma((groups,)),
            dma((groups, 2)),
            dma((sections,)),
            dma((groups, 2)),
            dma((groups, 2)),
            dma((sections, tiles)),
            dma((sections, tiles)),
            dma((2, tiles)),
            dma((2, tiles)),
            dma((groups, tiles)),
            dma((groups, tiles)),
            dma,
        ],
        compiler_params=pltpu.CompilerParams(collective_id=0, has_side_effects=True),
    )(probe, offsets, phase, absorption, measured)


def body(probe, offsets, phase, absorption, measured):
    sections, tiles = lax.axis_size("sec"), lax.axis_size("tile")
    if windowed(sections, tiles, *phase.shape, offsets.shape[0]):
        return windowed_body(sections, tiles, probe, offsets, phase, absorption, measured)
    return pipelined_body(probe, offsets, phase, absorption, measured)


def solution(mesh):
    in_specs = (
        P(None, "tile", None),
        P(),
        P("sec", "tile", None),
        P("sec", "tile", None),
        P(None, "tile", None),
    )
    out_specs = P("sec", None, "tile", None)
    return jax.shard_map(body, mesh=mesh, in_specs=in_specs, out_specs=out_specs, check_vma=False)
```

```python
import functools

import jax
import jax.numpy as jnp
from jax import lax
from jax.experimental import pallas as pl
from jax.experimental.pallas import tpu as pltpu
from jax.sharding import PartitionSpec as P

PROP_RE = 0.004
PROP_IM = 0.0314


def padded(value, sides, width):
    for axis, dim in sides:
        size, length = (lax.axis_size(axis), value.shape[dim])
        up = [(i, (i + 1) % size) for i in range(size - 1)]
        down = [(j, i) for i, j in up]
        last = lax.slice_in_dim(value, length - width, length, axis=dim)
        initial = lax.slice_in_dim(value, 0, width, axis=dim)
        before = lax.ppermute(last, axis, up)
        after = lax.ppermute(initial, axis, down)
        value = jnp.concatenate([before, value, after], axis=dim)
    return value


def passed_along(value, axis, steps):
    count = lax.axis_size(axis)
    initial, last = (max(0, -steps), min(count, count - steps))
    return lax.ppermute(value, axis, [(source, source + steps) for source in range(initial, last)])


def complex_product(multiplier, operand):
    real_part = (
        multiplier[..., 0, :, :] * operand[..., 0, :, :]
        - multiplier[..., 1, :, :] * operand[..., 1, :, :]
    )
    imag_part = (
        multiplier[..., 0, :, :] * operand[..., 1, :, :]
        + multiplier[..., 1, :, :] * operand[..., 0, :, :]
    )
    return jnp.stack([real_part, imag_part], -3)


def conjugate_product(multiplier, operand):
    real_part = (
        multiplier[..., 0, :, :] * operand[..., 0, :, :]
        + multiplier[..., 1, :, :] * operand[..., 1, :, :]
    )
    imag_part = (
        multiplier[..., 0, :, :] * operand[..., 1, :, :]
        - multiplier[..., 1, :, :] * operand[..., 0, :, :]
    )
    return jnp.stack([real_part, imag_part], -3)


def propagate(extended, coupling):
    centre = extended[..., 1:-1, :]
    laplacian = (
        extended[..., :-2, :]
        + extended[..., 2:, :]
        + jnp.roll(centre, 1, -1)
        + jnp.roll(centre, -1, -1)
        - 4.0 * centre
    )
    real_part = (
        centre[..., 0, :, :]
        + PROP_RE * laplacian[..., 0, :, :]
        - coupling * laplacian[..., 1, :, :]
    )
    imag_part = (
        centre[..., 1, :, :]
        + PROP_RE * laplacian[..., 1, :, :]
        + coupling * laplacian[..., 0, :, :]
    )
    return jnp.stack([real_part, imag_part], -3)


def forward_section(wavefield, transmission):
    slice_count = transmission.shape[0]
    inputs = []
    for layer_index in range(slice_count):
        inputs.append(wavefield)
        product = complex_product(transmission[layer_index], wavefield)
        extended = padded(product, (("tile", 2),), 1)
        wavefield = propagate(extended, PROP_IM)
    return (jnp.stack(inputs, 1), wavefield)


def backward_section(adjoint, inputs, weight, transmission):
    slice_count = transmission.shape[0]
    slice_grads = [None] * slice_count
    scaled = weight[:, None, None, None]
    for layer_index in reversed(range(slice_count)):
        extended = padded(adjoint, (("tile", 2),), 1)
        adjoint_wave = propagate(extended, -PROP_IM)
        slice_grads[layer_index] = jnp.sum(
            scaled * conjugate_product(inputs[:, layer_index], adjoint_wave), 0
        )
        adjoint = conjugate_product(transmission[layer_index], adjoint_wave)
    return (adjoint, jnp.stack(slice_grads, 0))


def pipelined_body(probe, offsets, phase, absorption, measured):
    slice_count, row_count, col_count = phase.shape
    amplitude = jnp.exp(-absorption)
    transmission = jnp.stack([amplitude * jnp.cos(phase), amplitude * jnp.sin(phase)], 1)
    sections = lax.axis_size("sec")
    section = lax.axis_index("sec")
    probe_count = offsets.shape[0]
    batch_size = 1
    step_count = sections + probe_count - 1

    def plan(step_index, offset_steps):
        raw_ids = (step_index - offset_steps)[None]
        active = (raw_ids >= 0) & (raw_ids < probe_count)
        return (jnp.clip(raw_ids, 0, probe_count - 1), active)

    def launch(shift_amount):
        return jnp.roll(probe, shift_amount, axis=-1)

    def forward_step(step_index, state_carry):
        incoming, stored, exit_waves = state_carry
        probe_ids, active = plan(step_index, section)
        launched = jax.vmap(launch)(offsets[probe_ids])
        wavefield = jnp.where(section == 0, launched, incoming)
        inputs, outgoing = forward_section(wavefield, transmission)
        stored = stored.at[probe_ids].set(
            jnp.where(active[:, None, None, None, None], inputs, stored[probe_ids])
        )
        exit_waves = exit_waves.at[probe_ids].set(
            jnp.where(active[:, None, None, None], outgoing, exit_waves[probe_ids])
        )
        incoming = passed_along(outgoing, "sec", 1)
        return (incoming, stored, exit_waves)

    zero_field = jnp.zeros((batch_size, 2, row_count, col_count), jnp.float32)
    stored = jnp.zeros((probe_count, slice_count, 2, row_count, col_count), jnp.float32)
    exit_waves = jnp.zeros((probe_count, 2, row_count, col_count), jnp.float32)
    unused, stored, exit_waves = lax.fori_loop(
        0, step_count, forward_step, (zero_field, stored, exit_waves)
    )

    def backward_step(step_index, state_carry):
        incoming, gradient = state_carry
        probe_ids, active = plan(step_index, sections - 1 - section)
        exit_part = exit_waves[probe_ids]
        intensity = exit_part[:, 0] ** 2 + exit_part[:, 1] ** 2
        seed_adjoint = 2.0 * (intensity - measured[probe_ids])[:, None] * exit_part
        adjoint = jnp.where(section == sections - 1, seed_adjoint, incoming)
        weight = active.astype(jnp.float32)
        adjoint, gradient_terms = backward_section(adjoint, stored[probe_ids], weight, transmission)
        incoming = passed_along(adjoint, "sec", -1)
        return (incoming, gradient + gradient_terms)

    gradient = jnp.zeros((slice_count, 2, row_count, col_count), jnp.float32)
    unused, gradient = lax.fori_loop(0, step_count, backward_step, (zero_field, gradient))
    return gradient


LANES = 128
SUBLANES = 8
DIRECT = 2
MESH = pl.DeviceIdType.MESH
CENTRE_RE = 1.0 - 4.0 * PROP_RE
CENTRE_IM = -4.0 * PROP_IM
RATIO = complex(PROP_RE, PROP_IM) / complex(CENTRE_RE, CENTRE_IM)


def windowed(sections, tiles, slice_count, row_count, col_count, probe_count):
    groups = col_count // LANES
    return (
        col_count % LANES == 0
        and groups >= 2
        and groups % 2 == 0
        and sections == 4 * groups
        and row_count % SUBLANES == 0
        and probe_count % tiles == 0
        and 2 * sections * slice_count <= LANES // 2
        and tiles * row_count <= 4 * SUBLANES
    )


def window_kernel(
    sections, tiles,
    probe_ref, offsets_ref, phase_ref, absorption_ref, measured_ref, out_ref,
    own, field, probes, frames, waves, adjoint, partial, returned, shifts,
    group_send, ready, plane_send, block_recv, corner_send, corner_recv,
    tile_send, tile_recv, aux_send, aux_recv, back_send, back_recv, shift_sem,
):
    slice_count, row_count, col_count = phase_ref.shape
    groups = col_count // LANES
    plane = sections // groups
    width = 2 * LANES
    height = tiles * row_count
    share = frames.shape[1]
    me = lax.axis_index("sec")
    tile = lax.axis_index("tile")
    group, place = lax.div(me, plane), lax.rem(me, plane)
    across = (place + 1 - 2 * lax.rem(place, 2), place + 2 - 4 * lax.div(place, 2))
    corner = plane - 1 - place

    def device(section, core):
        return {"sec": section, "tile": core}

    def group_at(step):
        return lax.rem(group + step, groups)

    def tile_at(step):
        return lax.rem(tile + step, tiles)

    def remote(source, target, send_sem, recv_sem, section, core):
        return pltpu.make_async_remote_copy(
            src_ref=source, dst_ref=target, send_sem=send_sem, recv_sem=recv_sem,
            device_id=device(section, core), device_id_type=MESH,
        )

    def arrived(target, recv_sem):
        remote(target, target, recv_sem, recv_sem, me, tile).wait_recv()

    shift_copy = pltpu.make_async_copy(offsets_ref, shifts, shift_sem)
    shift_copy.start()

    def greet(section, core):
        pl.semaphore_signal(
            pltpu.get_barrier_semaphore(), inc=1, device_id=device(section, core), device_id_type=MESH
        )

    for direction in (1, -1):
        @pl.when((group + direction >= 0) & (group + direction < groups))
        def _():
            greet(me + direction * plane, tile)
    for other in across:
        greet(group * plane + other, tile)
    for dj in range(1, tiles):
        greet(me, tile_at(dj))

    for layer in range(slice_count):
        amplitude = jnp.exp(-absorption_ref[layer])
        real = amplitude * jnp.cos(phase_ref[layer])
        imag = amplitude * jnp.sin(phase_ref[layer])
        for part, value in enumerate(
            (CENTRE_RE * real - CENTRE_IM * imag, CENTRE_RE * imag + CENTRE_IM * real)
        ):
            own[layer, part, :, :col_count] = value
            own[layer, part, :, col_count:] = value[:, :LANES]
    start = pl.multiple_of(group * LANES, LANES)
    field[me, tile] = own[:, :, :, pl.ds(start, width)]
    probes[tile] = probe_ref[...]
    frames[tile] = measured_ref[pl.ds(tile * share, share)]
    ends = lax.div(group + groups - 1, groups) + lax.div(2 * groups - 2 - group, groups)
    pl.semaphore_wait(pltpu.get_barrier_semaphore(), tiles - 1 + len(across) + ends)

    def group_copy(at, target):
        return remote(
            own.at[:, :, :, pl.ds(target * LANES, width)], field.at[me, tile], group_send.at[target],
            block_recv.at[me], me + (target - at) * plane, tile,
        )

    def tell(direction, distance):
        pl.semaphore_signal(
            ready.at[(direction + 1) // 2, distance], inc=1,
            device_id=device(me - direction * plane, tile), device_id_type=MESH,
        )

    def plane_copy(source, view, axis):
        block = source * plane + place
        return remote(
            view, field.at[block, tile], plane_send.at[source, axis], block_recv.at[block],
            group * plane + across[axis], tile,
        )

    def corner_copy(source, axis):
        part = field.at[source * plane + across[axis], tile, :, axis]
        return remote(
            part, part, corner_send.at[source, axis], corner_recv.at[source, axis],
            group * plane + across[1 - axis], tile,
        )

    def far_copy(source):
        view = field.at[source * plane + place, tile]
        return remote(
            view, view, corner_send.at[source, 0], corner_recv.at[source, 0],
            group * plane + corner, tile,
        )

    def tile_copies(block, view):
        return [
            remote(
                view, field.at[block, tile], tile_send.at[block, dj], tile_recv.at[block, tile],
                me, tile_at(dj),
            )
            for dj in range(1, tiles)
        ]

    def aux_copies():
        for dj in range(1, tiles):
            other = tile_at(dj)
            yield remote(
                probe_ref, probes.at[tile], aux_send.at[0, dj], aux_recv.at[0, tile], me, other
            )
            yield remote(
                measured_ref.at[pl.ds(other * share, share)], frames.at[tile], aux_send.at[1, dj],
                aux_recv.at[1, tile], me, other,
            )

    def launch():
        for dj in range(1, tiles):
            other = tile_at(dj)
            arrived(probes.at[other], aux_recv.at[0, other])
            arrived(frames.at[other], aux_recv.at[1, other])
        shift_copy.wait()
        for index in range(share):
            shift = lax.rem(shifts[tile * share + index] + col_count - group * LANES, col_count)
            for part in range(2):
                value = jnp.concatenate([probes[t, part] for t in range(tiles)], 0)
                for bit in range((col_count - 1).bit_length()):
                    chosen = jnp.full(value.shape, lax.shift_right_logical(shift, bit) & 1) == 1
                    value = jnp.where(chosen, pltpu.roll(value, 1 << bit, 1), value)
                waves[0, index, part] = value[:, :width]

    def ordered(at):
        return sorted(range(groups), key=lambda source: (abs(source - at), source))

    def gather(at):
        order = ordered(at)

        def reach(distance):
            for direction in (1, -1):
                target = at + direction * distance
                if 0 <= target < groups:
                    if distance > 1:
                        pl.semaphore_wait(ready.at[(direction + 1) // 2, distance], 1)
                    group_copy(at, target).start()
                    if 0 <= at - direction < groups:
                        tell(direction, distance + 1)

        def spread_out(source):
            view = field.at[source * plane + place, tile]
            for axis in range(2):
                plane_copy(source, view, axis).start()
            if source in order[groups - DIRECT:]:
                far_copy(source).start()
            for copy in tile_copies(source * plane + place, view):
                copy.start()

        def collect(source):
            for axis in range(2):
                block = source * plane + across[axis]
                arrived(field.at[block, tile], block_recv.at[block])
                if source not in order[groups - DIRECT:]:
                    corner_copy(source, axis).start()
                for copy in tile_copies(block, field.at[block, tile]):
                    copy.start()

        def collect_corner(source):
            block = source * plane + corner
            if source in order[groups - DIRECT:]:
                arrived(field.at[block, tile], corner_recv.at[source, 0])
            else:
                for axis in range(2):
                    arrived(field.at[block, tile, :, axis], corner_recv.at[source, axis])
            for copy in tile_copies(block, field.at[block, tile]):
                copy.start()

        reach(1)
        for count in range(groups + 2):
            if count < groups:
                source = order[count]
                if source != at:
                    block = source * plane + place
                    arrived(field.at[block, tile], block_recv.at[block])
                spread_out(source)
            if count == 0:
                for copy in aux_copies():
                    copy.start()
                for distance in range(2, groups):
                    reach(distance)
            if 0 <= count - 1 < groups:
                collect(order[count - 1])
            if 0 <= count - 2 < groups:
                collect_corner(order[count - 2])
            if count == 0:
                launch()

    for at in range(groups):
        @pl.when(group == at)
        def _():
            gather(at)

    rows = lax.broadcasted_iota(jnp.int32, (SUBLANES, width), 0)
    lanes = lax.broadcasted_iota(jnp.int32, (height, LANES), 1)
    first_row, last_row = rows == 0, rows == SUBLANES - 1
    first_lane, last_lane = lanes == 0, lanes == LANES - 1

    def neighbours(value):
        blocks = [value[at : at + SUBLANES] for at in range(0, height, SUBLANES)]
        down = [0.0] + [pltpu.roll(block, 1, 0) for block in blocks]
        up = [pltpu.roll(block, SUBLANES - 1, 0) for block in blocks] + [0.0]
        vertical = jnp.concatenate(
            [
                jnp.where(first_row, down[at], down[at + 1]) + jnp.where(last_row, up[at + 1], up[at])
                for at in range(len(blocks))
            ],
            0,
        )
        right = [pltpu.roll(value[:, at : at + LANES], 1, 1) for at in (0, LANES)]
        left = [pltpu.roll(value[:, at : at + LANES], LANES - 1, 1) for at in (0, LANES)]
        horizontal = jnp.concatenate(
            [
                right[0] + jnp.where(last_lane, left[1], left[0]),
                jnp.where(first_lane, right[0], right[1]) + left[1],
            ],
            1,
        )
        return vertical + horizontal

    def spread(real, imag, ratio):
        real_sum, imag_sum = neighbours(real), neighbours(imag)
        return (
            real + (ratio.real * real_sum - ratio.imag * imag_sum),
            imag + (ratio.real * imag_sum + ratio.imag * real_sum),
        )

    def layer_of(block, layer):
        return [
            jnp.concatenate([field[block, t, layer, part] for t in range(tiles)], 0)
            for part in range(2)
        ]

    def forward(block, carry):
        for dj in range(1, tiles):
            other = tile_at(dj)
            arrived(field.at[block, other], tile_recv.at[block, other])
        for layer in range(slice_count):
            at = block * slice_count + layer
            real, imag = layer_of(block, layer)
            for index in range(share):
                wave_re, wave_im = waves[at, index, 0], waves[at, index, 1]
                wave_re, wave_im = spread(
                    real * wave_re - imag * wave_im, real * wave_im + imag * wave_re, RATIO
                )
                waves[at + 1, index, 0] = wave_re
                waves[at + 1, index, 1] = wave_im
        return carry

    lax.fori_loop(0, sections, forward, 0)

    following = pl.multiple_of(group_at(1) * LANES, LANES)
    for index in range(share):
        frame = jnp.concatenate(
            [
                jnp.concatenate([frames[t, index, :, pl.ds(at, LANES)] for t in range(tiles)], 0)
                for at in (start, following)
            ],
            1,
        )
        wave_re, wave_im = (waves[sections * slice_count, index, part] for part in range(2))
        residual = 2.0 * (wave_re * wave_re + wave_im * wave_im - frame)
        adjoint[index, 0] = residual * wave_re
        adjoint[index, 1] = residual * wave_im

    def return_copy(piece, core):
        return pltpu.make_async_remote_copy(
            src_ref=partial.at[piece, core], dst_ref=returned.at[group, tile],
            send_sem=back_send.at[piece, core], recv_sem=back_recv.at[group, tile],
            device_id=device(piece * plane + place, core), device_id_type=MESH,
        )

    def backward(count, carry):
        block = sections - 1 - count
        piece = lax.div(block, plane)
        wanted = lax.rem(block, plane) == place
        for layer in reversed(range(slice_count)):
            at = block * slice_count + layer
            real, imag = layer_of(block, layer)
            backs = []
            for index in range(share):
                back_re, back_im = spread(adjoint[index, 0], adjoint[index, 1], RATIO.conjugate())
                backs.append((back_re, back_im))
                adjoint[index, 0] = real * back_re + imag * back_im
                adjoint[index, 1] = real * back_im - imag * back_re

            @pl.when(wanted)
            def _():
                total_re = total_im = 0.0
                for index, (back_re, back_im) in enumerate(backs):
                    wave_re, wave_im = waves[at, index, 0], waves[at, index, 1]
                    total_re += wave_re * back_re + wave_im * back_im
                    total_im += wave_re * back_im - wave_im * back_re
                for part, total in enumerate((total_re, total_im)):
                    chunk = pltpu.roll(total, width - LANES // 2, 1)[:, :LANES]
                    for core in range(tiles):
                        partial[piece, core, layer, part] = chunk[
                            core * row_count : (core + 1) * row_count
                        ]

        for core in range(tiles):
            @pl.when(wanted & (piece * tiles + core != group * tiles + tile))
            def _():
                return_copy(piece, core).start()

        return carry

    lax.fori_loop(0, sections - place, backward, 0)

    returned[group, tile] = partial[group, tile]
    for dz in range(groups):
        for dj in range(tiles):
            if dz or dj:
                piece, core = group_at(dz), tile_at(dj)
                arrived(returned.at[piece, core], back_recv.at[piece, core])
    for layer in range(slice_count):
        parts = []
        for part in range(2):
            chunks = []
            for piece in range(groups):
                chunk = returned[piece, 0, layer, part]
                for core in range(1, tiles):
                    chunk = chunk + returned[piece, core, layer, part]
                chunks.append(chunk)
            parts.append(pltpu.roll(jnp.concatenate(chunks, 1), LANES // 2, 1))
        real, imag = parts
        out_ref[layer, 0] = CENTRE_RE * real + CENTRE_IM * imag
        out_ref[layer, 1] = CENTRE_RE * imag - CENTRE_IM * real

    for dz in range(groups):
        for dj in range(tiles):
            if dz or dj:
                return_copy(group_at(dz), tile_at(dj)).wait_send()
    for at in range(groups):
        @pl.when(group == at)
        def _():
            for target in range(groups):
                if target != at:
                    group_copy(at, target).wait_send()
            for count, source in enumerate(ordered(at)):
                if count >= groups - DIRECT:
                    far_copy(source).wait_send()
                else:
                    for axis in range(2):
                        corner_copy(source, axis).wait_send()
    for source in range(groups):
        for axis in range(2):
            plane_copy(source, field.at[source * plane + place, tile], axis).wait_send()
    for block in range(sections):
        for copy in tile_copies(block, field.at[block, tile]):
            copy.wait_send()
    for copy in aux_copies():
        copy.wait_send()


def windowed_body(sections, tiles, probe, offsets, phase, absorption, measured):
    slice_count, row_count, col_count = phase.shape
    probe_count = offsets.shape[0]
    groups = col_count // LANES
    plane = sections // groups
    width, height, share = 2 * LANES, tiles * row_count, probe_count // tiles
    vmem = pl.BlockSpec(memory_space=pltpu.VMEM)
    dma = pltpu.SemaphoreType.DMA
    return pl.pallas_call(
        functools.partial(window_kernel, sections, tiles),
        out_shape=jax.ShapeDtypeStruct((slice_count, 2, row_count, col_count), jnp.float32),
        in_specs=[vmem, pl.BlockSpec(memory_space=pl.ANY), vmem, vmem, vmem],
        out_specs=vmem,
        scratch_shapes=[
            pltpu.VMEM((slice_count, 2, row_count, col_count + LANES), jnp.float32),
            pltpu.VMEM((sections, tiles, slice_count, 2, row_count, width), jnp.float32),
            pltpu.VMEM((tiles, 2, row_count, col_count), jnp.float32),
            pltpu.VMEM((tiles, share, row_count, col_count), jnp.float32),
            pltpu.VMEM((sections * slice_count + 1, share, 2, height, width), jnp.float32),
            pltpu.VMEM((share, 2, height, width), jnp.float32),
            pltpu.VMEM((groups, tiles, slice_count, 2, row_count, LANES), jnp.float32),
            pltpu.VMEM((groups, tiles, slice_count, 2, row_count, LANES), jnp.float32),
            pltpu.SMEM((probe_count,), jnp.int32),
            dma((groups,)),
            pltpu.SemaphoreType.REGULAR((2, groups)),
            dma((groups, 2)),
            dma((sections,)),
            dma((groups, 2)),
            dma((groups, 2)),
            dma((sections, tiles)),
            dma((sections, tiles)),
            dma((2, tiles)),
            dma((2, tiles)),
            dma((groups, tiles)),
            dma((groups, tiles)),
            dma,
        ],
        compiler_params=pltpu.CompilerParams(collective_id=0, has_side_effects=True),
    )(probe, offsets, phase, absorption, measured)


def body(probe, offsets, phase, absorption, measured):
    sections, tiles = lax.axis_size("sec"), lax.axis_size("tile")
    if windowed(sections, tiles, *phase.shape, offsets.shape[0]):
        return windowed_body(sections, tiles, probe, offsets, phase, absorption, measured)
    return pipelined_body(probe, offsets, phase, absorption, measured)


def solution(mesh):
    in_specs = (
        P(None, "tile", None),
        P(),
        P("sec", "tile", None),
        P("sec", "tile", None),
        P(None, "tile", None),
    )
    out_specs = P("sec", None, "tile", None)
    return jax.shard_map(body, mesh=mesh, in_specs=in_specs, out_specs=out_specs, check_vma=False)
```
